256 devices in a mesh: tile: 64 (over x, y, z_lo), slab: 4 (over z_hi, core).
Axes of the slice: x: 4, y: 4, z: 8 (z_hi: 2, z_lo: 4; z = z_hi * 4 + z_lo), core: 2. Of those that a mesh axis runs over, the one named last changes fastest.
Arguments:
- kernels: float32 [64, 3, 64, 128, 128], P('tile', None, 'slab'), may hold values from -60 to 60
- volume: float32 [64, 64, 128, 128], P('tile', 'slab'), may hold values from 0.25 to 4
- neighbours: int32 [64, 4], replicated, may hold values from 0 to 63, as said below
- glued_sides: int32 [64, 4], replicated, may hold values from 0 to 3
- reversals: int32 [64, 4], replicated, may hold values from 0 to 1, as said below
Outputs:
- smoothed: float32 [64, 3, 64, 128, 128], P('tile', None, 'slab')
The draws below stay inside these ranges and needn't reach their ends.
Inputs may be any that keep to these rules, and one draw needn't show every extreme that they name: Each side of each tile is glued to exactly one side of some tile (possibly another side of the same tile), and the gluing is symmetric: side glued_sides[t, s] of tile neighbours[t, s] is glued back to side s of tile t. The gluing is known only at run time. `reversals`: the two sides of a glued pair carry the same code.
All inputs are finite; a program needn't handle non-finite values.
Results may differ from the reference program's by a relative error of at most 0.000073.
Values sent between devices are 32-bit elements; how exact they have to be, the bound alone decides.
No kernel may reach another device: no remote copies, remote signals or barrier semaphores. Data moves between devices by JAX's collectives and lax.ppermute only.
A program may use at most 128 MiB of HBM per device.

```python
import math
import jax
import jax.numpy as jnp
from jax import lax

SIDE = 128
LEVELS = 64
FIELDS = 3
HALF = 15
TILES = 64


def gluing(key):
    base_key = jax.random.fold_in(key, 7)
    order = jax.random.permutation(jax.random.fold_in(base_key, 1), 4 * TILES).astype(jnp.int32)
    paired = order.reshape(2 * TILES, 2)
    partner = jnp.zeros((4 * TILES,), jnp.int32)
    partner = partner.at[paired[:, 0]].set(paired[:, 1]).at[paired[:, 1]].set(paired[:, 0])
    coins = jax.random.randint(jax.random.fold_in(base_key, 2), (2 * TILES,), 0, 2).astype(jnp.int32)
    coins = coins.at[0].set(1).at[1].set(0)
    flipped = jnp.zeros((4 * TILES,), jnp.int32)
    flipped = flipped.at[paired[:, 0]].set(coins).at[paired[:, 1]].set(coins)
    return (partner.reshape(TILES, 4), flipped.reshape(TILES, 4))


def draw_neighbours(key, part):
    partner, flipped = gluing(key)
    return partner // 4


def draw_glued_sides(key, part):
    partner, flipped = gluing(key)
    return partner % 4


def draw_reversals(key, part):
    partner, flipped = gluing(key)
    return flipped


def block_scale(key, extent, shards, smallest, top_value):
    def one(dim, blocks):
        heights = jax.random.uniform(jax.random.fold_in(jax.random.fold_in(key, 6), dim), (blocks,), jnp.float32, smallest / len(shards), top_value / len(shards))
        return jnp.repeat(jnp.exp(heights), extent[dim] // blocks).reshape((-1,) + (1,) * (len(extent) - dim - 1))

    loudness = one(*shards[0])
    for cut in shards[1:]:
        loudness = loudness * one(*cut)
    return loudness


def setup_inputs(seed: int = 0) -> dict:
    key_of = jax.random.split(jax.random.key(seed), 6)
    return {
        "kernels": jnp.clip(jax.random.uniform(key_of[0], (TILES, FIELDS, LEVELS, SIDE, SIDE), jnp.float32, -60.0, 60.0) * block_scale(key_of[0], (TILES, FIELDS, LEVELS, SIDE, SIDE), ((0, 64), (2, 4)), -0.4, 0.0), -60.0, 60.0),
        "volume": jnp.clip(jnp.exp(math.log(4.0) - 2.7725887 * jax.random.uniform(key_of[1], (TILES, LEVELS, SIDE, SIDE), jnp.float32) ** block_scale(key_of[1], (TILES, LEVELS, SIDE, SIDE), ((0, 64), (1, 4)), -0.2, 0.2)), 0.25, 4.0),
        "neighbours": draw_neighbours(jax.random.fold_in(key_of[5], 71), 0),
        "glued_sides": draw_glued_sides(jax.random.fold_in(key_of[5], 71), 0),
        "reversals": draw_reversals(jax.random.fold_in(key_of[5], 71), 0),
    }


spread_cells = 5.0


def gaussian(height, breadth, centre):
    row_index = lax.broadcasted_iota(jnp.int32, (height, breadth), 0)
    col_index = lax.broadcasted_iota(jnp.int32, (height, breadth), 1)
    offset = (row_index - col_index - centre).astype(jnp.float32)
    weights = jnp.exp(-offset * offset / (2.0 * spread_cells * spread_cells))
    return jnp.where(jnp.abs(offset) <= HALF, weights, jnp.zeros_like(weights))


def edge_strips(values):
    west_part = jnp.swapaxes(values[..., :HALF], -1, -2)
    east_part = jnp.swapaxes(values[..., ::-1][..., :HALF], -1, -2)
    south_part = values[..., :HALF, :]
    north_part = values[..., ::-1, :][..., :HALF, :]
    return jnp.stack([west_part, east_part, south_part, north_part], axis=1)


def route_strips(strips, neighbours, glued_sides, reversals):
    flattened = strips.reshape((strips.shape[0] * 4,) + strips.shape[2:])
    picked = flattened[(neighbours * 4 + glued_sides).reshape(-1)]
    picked = picked.reshape((neighbours.shape[0], 4) + strips.shape[2:])
    return jnp.where(reversals[:, :, None, None, None] == 1, picked[..., ::-1], picked)


def pass_across(values, halo_cells):
    side_cells = values.shape[-1]
    west_part = jnp.swapaxes(halo_cells[0], -1, -2)[..., ::-1]
    east_part = jnp.swapaxes(halo_cells[1], -1, -2)
    padded = jnp.concatenate([west_part, values, east_part], axis=-1)
    weights = gaussian(side_cells + 2 * HALF, side_cells, HALF)
    return jnp.einsum('qyp,px->qyx', padded, weights, precision=lax.Precision.HIGHEST)


def pass_along(values, halo_cells):
    side_cells = values.shape[-1]
    south_part = halo_cells[2][:, ::-1, :]
    padded = jnp.concatenate([south_part, values, halo_cells[3]], axis=1)
    weights = gaussian(side_cells + 2 * HALF, side_cells, HALF)
    return jnp.einsum('qpx,py->qyx', padded, weights, precision=lax.Precision.HIGHEST)


def reference(kernels, volume, neighbours, glued_sides, reversals):
    tile_count = kernels.shape[0]
    field_count = kernels.shape[1]
    level_count = kernels.shape[2]
    side_cells = kernels.shape[3]
    stacked = jnp.concatenate([kernels * volume[:, None], volume[:, None]], axis=1)
    row_stack = stacked.reshape(tile_count, -1, side_cells, side_cells)
    halo_cells = route_strips(edge_strips(row_stack), neighbours, glued_sides, reversals)
    across = lax.map(lambda element: pass_across(element[0], element[1]), (row_stack, halo_cells))
    halo_cells = route_strips(edge_strips(across), neighbours, glued_sides, reversals)
    lateral = lax.map(lambda element: pass_along(element[0], element[1]), (across, halo_cells))
    lateral = lateral.reshape(tile_count, field_count + 1, level_count, side_cells, side_cells)
    radial_weights = gaussian(level_count, level_count, 0)

    def normalise(column_block):
        smooth = jnp.einsum('lm,flyx->fmyx', radial_weights, column_block, precision=lax.Precision.HIGHEST)
        return smooth[:-1] / smooth[-1:]

    return lax.map(normalise, lateral)
```

```python
import functools
import math

import jax
import jax.numpy as jnp
import numpy as np
from jax import lax
from jax.experimental import pallas as pl
from jax.experimental.pallas import tpu as pltpu
from jax.sharding import PartitionSpec as P

SIDE = 128
HALF = 15
DEEP = 16
OWN = 16
SPAN = 2 * HALF + OWN
F32 = jnp.float32
BF16 = jnp.bfloat16

TAPS = [float(np.float32(math.exp(-k * k / 50.0))) for k in range(HALF + 1)]


def tap(offset):
    offset = np.abs(np.asarray(offset))
    return np.where(offset <= HALF, np.exp(-(offset.astype(np.float64) ** 2) / 50.0), 0.0).astype(np.float32)


def halves(values):
    high = values.astype(BF16)
    low = (values - high.astype(np.float32)).astype(BF16)
    return high, low


def constants():
    cell = np.arange(SIDE)
    deep = np.arange(DEEP)
    live = (deep < HALF)[:, None]
    square = tap(cell[:, None] - cell[None, :])
    high, low = halves(square)
    pair = np.block([[high, low], [high, np.zeros_like(low)]])
    near = tap(cell[None, :] + deep[:, None] + 1) * live
    far = tap(SIDE - cell[None, :] + deep[:, None]) * live
    pick_west = (cell[None, :] == deep[:, None]).astype(np.float32) * live
    pick_east = (cell[None, :] == SIDE - 1 - deep[:, None]).astype(np.float32) * live
    sum_west = tap(cell[None, :] - deep[:, None]) * live
    sum_east = tap(cell[None, :] - (SIDE - 1 - deep[:, None])) * live
    picks = np.stack([pick_west, pick_east, sum_west, sum_east])
    back = tap(deep[:, None] + deep[None, :] + 1) * live * live.T
    south_own = near.T.astype(np.float64) @ back
    north_own = (far.T.astype(np.float64) @ back)[:, ::-1]
    along = np.concatenate([square, near.T, far.T, south_own, north_own], axis=1).astype(np.float32)
    eye = np.eye(8, dtype=np.float32)
    spread = np.concatenate([np.kron(eye, near), np.kron(eye, far)], axis=0)
    corner = np.kron(np.eye(4, dtype=np.float32), np.concatenate([near, far], axis=0))
    ends = np.concatenate([pick_west, pick_east], axis=0)
    return dict(
        pair=pair,
        picks=picks,
        along=along,
        spread=np.stack(halves(spread)),
        corner=np.stack(halves(corner)),
        ends=ends.astype(BF16),
    )


def split(values):
    high = values.astype(BF16)
    return high, (values - high.astype(F32)).astype(BF16)


def dot(left, right):
    return jnp.dot(left, right, preferred_element_type=F32)


def dot_t(left, right):
    return lax.dot_general(left, right, (((1,), (1,)), ((), ())), preferred_element_type=F32)


def through(rows, pair):
    high, low = split(rows)
    both = dot(jnp.concatenate([high, low], axis=1), pair)
    return both[:, :SIDE] + both[:, SIDE:]


def radial_kernel(weighted, *refs):
    out = refs[-1]
    parts = refs[:-1]
    rows = out.shape[1]

    def tile(i, carry):
        at = pl.ds(pl.multiple_of(i * 8, 8), 8)

        def level(j):
            part, k = (0, j) if j < HALF else (1, j - HALF) if j < HALF + OWN else (2, j - HALF - OWN)
            x = parts[part][k, at, :]
            return x * parts[part + 3][k, at, :] if weighted else x

        x = [level(j) for j in range(SPAN)]
        for m in range(OWN):
            c = m + HALF
            total = TAPS[0] * x[c]
            for k in range(1, HALF + 1):
                total = total + TAPS[k] * (x[c - k] + x[c + k])
            out[m, at, :] = total
        return carry

    lax.fori_loop(0, rows // 8, tile, 0)


def radial(parts, weights):
    weighted = weights is not None
    arrays = list(parts) + (list(weights) if weighted else [])
    block = 32
    return pl.pallas_call(
        functools.partial(radial_kernel, weighted),
        grid=(SIDE // block,),
        in_specs=[pl.BlockSpec((a.shape[0], block, SIDE), lambda i: (0, i, 0)) for a in arrays],
        out_specs=pl.BlockSpec((OWN, block, SIDE), lambda i: (0, i, 0)),
        out_shape=jax.ShapeDtypeStruct((OWN, SIDE, SIDE), F32),
        name="radial",
        cost_estimate=pl.CostEstimate(flops=OWN * SPAN * SIDE * SIDE * 2, bytes_accessed=7 << 20, transcendentals=0),
    )(*arrays)


def pack_kernel(field_count, glued, pair, picks, *refs):
    fields = refs[:field_count]
    out, edge = refs[field_count:]

    def choose(side):
        raw = jnp.where(glued[side] < 2, 1.0, 0.0).astype(F32)
        return picks[side] * raw + picks[side + 2] * (1.0 - raw)

    left_high, left_low = split(jnp.concatenate([choose(0), choose(1)], axis=0))
    left = jnp.concatenate([left_high, left_low], axis=0)
    for f in range(field_count):
        rows = fields[f]
        mine = pl.ds(f * OWN, OWN)
        for d in range(DEEP):
            edge[pl.ds(d, OWN, stride=DEEP), :] = rows[pl.ds(d, OWN, stride=SIDE), :]
            edge[pl.ds(OWN * DEEP + d, OWN, stride=DEEP), :] = rows[pl.ds(SIDE - 1 - d, OWN, stride=SIDE), :]
        raw = edge[...]
        across = through(raw, pair[...])
        for side in (2, 3):
            at = slice((side - 2) * OWN * DEEP, (side - 1) * OWN * DEEP)
            strip = jnp.where(glued[side] < 2, raw[at], across[at])
            out[mine, side, :, :] = strip.reshape(OWN, DEEP, SIDE)
        high, low = split(rows[...])
        both = dot_t(left, high)
        strips = both[: 2 * DEEP] + both[2 * DEEP :] + dot_t(left_high, low)
        for q in range(OWN):
            plane = strips[:, q * SIDE : (q + 1) * SIDE]
            out[f * OWN + q, 0, :, :] = plane[:DEEP]
            out[f * OWN + q, 1, :, :] = plane[DEEP:]


VMEM = pl.BlockSpec(memory_space=pltpu.VMEM)
SMEM = pl.BlockSpec(memory_space=pltpu.SMEM)


def pack(fields, glued, const):
    count = len(fields)
    return pl.pallas_call(
        functools.partial(pack_kernel, count),
        in_specs=[SMEM] + [VMEM] * (2 + count),
        out_specs=VMEM,
        out_shape=jax.ShapeDtypeStruct((count * OWN, 4, DEEP, SIDE), F32),
        scratch_shapes=[pltpu.VMEM((2 * OWN * DEEP, SIDE), F32)],
        name="pack",
        cost_estimate=pl.CostEstimate(flops=1 << 29, bytes_accessed=6 << 20, transcendentals=0),
    )(glued, const["pair"], const["picks"], *[f.reshape(OWN * SIDE, SIDE) for f in fields])


def route_kernel(source, fix, ends, corner, flipped, strips, out, patch):
    tiles = out.shape[0]
    group = 4

    def move(i, carry):
        for j in range(8):
            e = i * 8 + j
            t, s = i * 2 + j // 4, j % 4
            out[t, s, :, :] = strips[source[e], :, :]
        return carry

    lax.fori_loop(0, tiles // 2, move, 0)
    margins = out[:, 0:2, :, :].reshape(tiles * 2 * DEEP, SIDE)
    high, low = split(margins)
    seen = dot_t(ends[...], high) + dot_t(ends[...], low)
    first, last = seen[:DEEP], seen[DEEP:]
    swap = flipped[...] > 0.5
    turned = jnp.concatenate([jnp.where(swap, last, first), jnp.where(swap, first, last)], axis=0)
    high, low = split(turned)
    for g in range(tiles // group):
        at = slice(g * SIDE, (g + 1) * SIDE)
        added = dot(high[:, at], corner[0]) + dot(high[:, at], corner[1]) + dot(low[:, at], corner[0])
        for j in range(group):
            block = added[:, j * SIDE : (j + 1) * SIDE]
            patch[(g * group + j) * 2] = block[:DEEP]
            patch[(g * group + j) * 2 + 1] = block[DEEP:]
    patch[tiles * 2] = jnp.zeros((DEEP, SIDE), F32)

    def mend(i, carry):
        for j in range(4):
            t, s = i * 2 + j // 2, 2 + j % 2
            out[t, s, :, :] = out[t, s, :, :] + patch[fix[i * 4 + j], :, :]
        return carry

    lax.fori_loop(0, tiles // 2, mend, 0)


def route(strips, tables, const):
    tiles = strips.shape[0]
    source, fix, flipped = tables
    return pl.pallas_call(
        route_kernel,
        in_specs=[SMEM, SMEM] + [VMEM] * 4,
        out_specs=VMEM,
        out_shape=jax.ShapeDtypeStruct((tiles, 4, DEEP, SIDE), F32),
        scratch_shapes=[pltpu.VMEM((tiles * 2 + 1, DEEP, SIDE), F32)],
        name="route",
        cost_estimate=pl.CostEstimate(flops=1 << 28, bytes_accessed=4 << 20, transcendentals=0),
    )(source, fix, const["ends"], const["corner"], flipped, strips.reshape(tiles * 4, DEEP, SIDE))


def turn(code):
    row = lax.broadcasted_iota(jnp.int32, (SIDE, SIDE), 0)
    col = lax.broadcasted_iota(jnp.int32, (SIDE, SIDE), 1)
    return jnp.where(col == jnp.where(code == 1, SIDE - 1 - row, row), 1.0, 0.0).astype(BF16)


def finish_kernel(glued, turned, pair, along, spread, margins, *refs):
    fields = refs[:4]
    out, rows, across, below = refs[4:]
    f = pl.program_id(0)
    for k in range(4):

        @pl.when(f == k)
        def _():
            rows[...] = fields[k][...]

    size = OWN * DEEP
    across[...] = through(rows[...], pair[...]).reshape(OWN, SIDE, SIDE)
    sides = []
    for side in (0, 1):
        high, low = split(margins[:, side, :, :].reshape(size, SIDE))
        way = turn(turned[side])
        sides.append(dot_t(way, high) + dot_t(way, low))
    for g in range(2):
        at = slice(g * SIDE, (g + 1) * SIDE)
        high, low = split(jnp.concatenate([sides[0][:, at], sides[1][:, at]], axis=1))
        for q in range(0, 8, 2):
            to = slice(q * SIDE, (q + 2) * SIDE)
            added = dot(high, spread[0, :, to]) + dot(high, spread[1, :, to]) + dot(low, spread[0, :, to])
            across[g * 8 + q] += added[:, :SIDE]
            across[g * 8 + q + 1] += added[:, SIDE:]
    ahead = []
    for side in (2, 3):
        high, low = split(margins[:, side, :, :].reshape(size, SIDE))
        way = turn(turned[side])
        ahead.append((dot(high, way) + dot(low, way)).reshape(OWN, DEEP, SIDE))
    lane = lax.broadcasted_iota(jnp.int32, (SIDE, along.shape[1]), 1)
    south = jnp.where(glued[2] < 2, 1.0, 0.0).astype(F32)
    north = jnp.where(glued[3] < 2, 1.0, 0.0).astype(F32)
    first_own = SIDE + 2 * DEEP
    scale = jnp.where(lane < first_own, 1.0, jnp.where(lane < first_own + DEEP, south, north))
    left_high, left_low = split(along[...] * scale)
    left = jnp.concatenate([left_high, left_low], axis=0)

    def column(q):
        base = q * SIDE
        return jnp.concatenate(
            [across[q], ahead[0][q], ahead[1][q], rows[base : base + DEEP, :], rows[base + SIDE - DEEP : base + SIDE, :]],
            axis=0,
        )

    for q in range(0, OWN, 2):
        high, low = split(jnp.concatenate([column(q), column(q + 1)], axis=1))
        both = dot(left, high)
        total = both[:SIDE] + both[SIDE:] + dot(left_high, low)
        for j in range(2):
            plane = total[:, j * SIDE : (j + 1) * SIDE]

            @pl.when(f == 0)
            def _():
                below[q + j] = plane

            @pl.when(f > 0)
            def _():
                out[0, q + j] = plane / below[q + j]


def finish(fields, margins, glued, turned, const):
    whole = [pl.BlockSpec((OWN * SIDE, SIDE), lambda i: (0, 0)) for _ in range(4)]
    return pl.pallas_call(
        finish_kernel,
        grid=(4,),
        in_specs=[SMEM, SMEM]
        + [
            pl.BlockSpec(const["pair"].shape, lambda i: (0, 0)),
            pl.BlockSpec(const["along"].shape, lambda i: (0, 0)),
            pl.BlockSpec(const["spread"].shape, lambda i: (0, 0, 0)),
            pl.BlockSpec((OWN, 4, DEEP, SIDE), lambda i: (i, 0, 0, 0)),
        ]
        + whole,
        out_specs=pl.BlockSpec((1, OWN, SIDE, SIDE), lambda i: (jnp.maximum(i - 1, 0), 0, 0, 0)),
        out_shape=jax.ShapeDtypeStruct((3, OWN, SIDE, SIDE), F32),
        scratch_shapes=[
            pltpu.VMEM((OWN * SIDE, SIDE), F32),
            pltpu.VMEM((OWN, SIDE, SIDE), F32),
            pltpu.VMEM((OWN, SIDE, SIDE), F32),
        ],
        name="finish",
        cost_estimate=pl.CostEstimate(flops=1 << 32, bytes_accessed=10 << 20, transcendentals=0),
    )(
        glued,
        turned,
        const["pair"],
        const["along"],
        const["spread"],
        margins,
        *[f.reshape(OWN * SIDE, SIDE) for f in fields],
    )


UP = [(0, 1), (1, 2), (2, 3)]
DOWN = [(1, 0), (2, 1), (3, 2)]


def with_halo(levels):
    below = lax.ppermute(levels[1:], "slab", UP)
    above = lax.ppermute(levels[:-1], "slab", DOWN)
    return below, levels, above


def per_device(kernels, volume, neighbours, glued_sides, reversals):
    const = {k: jnp.asarray(v) for k, v in constants().items()}
    tile = lax.axis_index("tile")
    glued = glued_sides[tile]
    turned = reversals[tile]
    tiles = neighbours.shape[0]
    source = (neighbours * 4 + glued_sides).reshape(-1)
    ahead = glued_sides[:, 2:]
    fix = jnp.where(ahead >= 2, neighbours[:, 2:] * 2 + ahead - 2, tiles * 2).reshape(-1)
    flipped = jnp.repeat(reversals[:, :2].astype(F32).reshape(-1), DEEP)[None, :]
    tables = (source, fix, flipped)

    weights = with_halo(volume[0])
    fields = [radial(weights, None)]
    for f in range(3):
        fields.append(radial(with_halo(kernels[0, f]), weights))
    strips = pack(fields, glued, const)
    routed_in = lax.all_to_all(strips, "tile", split_axis=0, concat_axis=0, tiled=True)
    picked = route(routed_in, tables, const)
    margins = lax.all_to_all(picked, "tile", split_axis=0, concat_axis=0, tiled=True)
    return finish(fields, margins, glued, turned, const)[None]


def solution(mesh):
    placed = (P("tile", None, "slab", None, None), P("tile", "slab", None, None), P(), P(), P())
    return jax.shard_map(
        per_device,
        mesh=mesh,
        in_specs=placed,
        out_specs=P("tile", None, "slab", None, None),
        check_vma=False,
    )
```

```python
import functools
import math

import jax
import jax.numpy as jnp
import numpy as np
from jax import lax
from jax.experimental import pallas as pl
from jax.experimental.pallas import tpu as pltpu
from jax.sharding import PartitionSpec as P


SIDE = 128
HALF = 15
DEEP = 16
OWN = 16
SPAN = 2 * HALF + OWN
F32 = jnp.float32
BF16 = jnp.bfloat16

ROOM = pltpu.CompilerParams(vmem_limit_bytes=24 << 20)
TAPS = [float(np.float32(math.exp(-k * k / 50.0))) for k in range(HALF + 1)]


def tap(offset):
    offset = np.abs(np.asarray(offset))
    return np.where(offset <= HALF, np.exp(-(offset.astype(np.float64) ** 2) / 50.0), 0.0).astype(np.float32)


def halves(values):
    high = values.astype(BF16)
    low = (values - high.astype(np.float32)).astype(BF16)
    return high, low


def constants():
    cell = np.arange(SIDE)
    deep = np.arange(DEEP)
    live = (deep < HALF)[:, None]
    square = tap(cell[:, None] - cell[None, :])
    high, low = halves(square)
    pair = np.block([[high, low], [high, np.zeros_like(low)]])
    near = tap(cell[None, :] + deep[:, None] + 1) * live
    far = tap(SIDE - cell[None, :] + deep[:, None]) * live
    pick_west = (cell[None, :] == deep[:, None]).astype(np.float32) * live
    pick_east = (cell[None, :] == SIDE - 1 - deep[:, None]).astype(np.float32) * live
    sum_west = tap(cell[None, :] - deep[:, None]) * live
    sum_east = tap(cell[None, :] - (SIDE - 1 - deep[:, None])) * live
    picks = np.stack([pick_west, pick_east, sum_west, sum_east])
    back = tap(deep[:, None] + deep[None, :] + 1) * live * live.T
    south_own = near.T.astype(np.float64) @ back
    north_own = (far.T.astype(np.float64) @ back)[:, ::-1]
    along = np.concatenate([square, south_own, north_own], axis=1).astype(np.float32)
    ahead_high, ahead_low = halves(np.concatenate([near.T, far.T], axis=1))
    eye = np.eye(4, dtype=np.float32)
    spread_high, spread_low = halves(np.concatenate([np.kron(eye, near), np.kron(eye, far)], axis=0))
    corner = np.kron(eye, np.concatenate([near, far], axis=0))
    ends = np.concatenate([pick_west, pick_east], axis=0)
    return dict(
        pair=pair,
        picks=picks,
        along=along,
        square=np.stack([high, low]),
        ahead=np.concatenate([ahead_high, ahead_high, ahead_low], axis=1),
        spread=np.concatenate([spread_high, spread_high, spread_low], axis=0),
        corner=np.stack(halves(corner)),
        ends=ends.astype(BF16),
    )


def split(values):
    high = values.astype(BF16)
    return high, (values - high.astype(F32)).astype(BF16)


def dot(left, right):
    return jnp.dot(left, right, preferred_element_type=F32)


def dot_t(left, right):
    return lax.dot_general(left, right, (((1,), (1,)), ((), ())), preferred_element_type=F32)


def through(rows, pair):
    high, low = split(rows)
    both = dot(jnp.concatenate([high, low], axis=1), pair)
    return both[:, :SIDE] + both[:, SIDE:]


VMEM = pl.BlockSpec(memory_space=pltpu.VMEM)
SMEM = pl.BlockSpec(memory_space=pltpu.SMEM)


PAIRS = 48
RIM = 2 * DEEP + PAIRS
QUARTER = SIDE // 4
UPPER = DEEP + PAIRS


def lanes(shape):
    return lax.broadcasted_iota(jnp.int32, shape, len(shape) - 1)


def rolled(x, amount):
    return pltpu.roll(x, amount, x.ndim - 1)


def two(first, second):
    return jnp.where(lanes(first.shape) < SIDE // 2, first, second)


def rim_pairs(first, second):
    return two(rolled(first, QUARTER), rolled(second, 3 * QUARTER))


def core_pairs(first, second):
    return two(rolled(first, 3 * QUARTER), rolled(second, QUARTER))


def unpair(rim, core):
    edge = lanes(rim.shape)
    edge = (edge < QUARTER) | (edge >= 3 * QUARTER)
    inside = (rolled(core, QUARTER), rolled(core, 3 * QUARTER)) if core is not None else (0.0, 0.0)
    return jnp.where(edge, rolled(rim, 3 * QUARTER), inside[0]), jnp.where(edge, rolled(rim, QUARTER), inside[1])


def levels_out(l, value, at, own, up, down):
    own[l, at, :] = value
    if l > 0:
        up[l - 1, at, :] = value
    if l < OWN - 1:
        down[l, at, :] = value


def rim_kernel(weighted, *refs):
    outs = refs[2 if weighted else 1 :]
    for l in range(OWN):

        def rows(start, count):
            x = refs[0][0, l, start : start + count, :]
            return x * refs[1][0, l, start : start + count, :] if weighted else x

        levels_out(l, rows(0, DEEP), slice(0, DEEP), *outs)
        levels_out(l, rows(SIDE - DEEP, DEEP), slice(DEEP, 2 * DEEP), *outs)
        levels_out(l, rim_pairs(rows(DEEP, PAIRS), rows(UPPER, PAIRS)), slice(2 * DEEP, RIM), *outs)


def rim_of(kernels, volume, field):
    arrays = [volume] if field is None else [kernels, volume]
    spec = [pl.BlockSpec((1, OWN, SIDE, SIDE), lambda i: (0, 0, 0, 0))]
    if field is not None:
        spec = [pl.BlockSpec((1, OWN, SIDE, SIDE), lambda i: (field, 0, 0, 0))] + spec
    shapes = [jax.ShapeDtypeStruct((count, RIM, SIDE), F32) for count in (OWN, OWN - 1, OWN - 1)]
    return pl.pallas_call(
        functools.partial(rim_kernel, field is not None),
        grid=(1,),
        in_specs=spec,
        out_specs=[pl.BlockSpec(x.shape, lambda i: (0, 0, 0)) for x in shapes],
        out_shape=shapes,
        name="rim",
        compiler_params=ROOM,
        cost_estimate=pl.CostEstimate(flops=1 << 20, bytes_accessed=4 << 20, transcendentals=0),
    )(*arrays)


def core_kernel(kernels, volume, own, up, down):
    field = jnp.full((PAIRS, SIDE), pl.program_id(0), jnp.int32)
    for l in range(OWN):
        parts = []
        for start in (DEEP, UPPER):
            w = volume[l, start : start + PAIRS, :]
            parts.append(jnp.where(field == 0, w, w * kernels[0, l, start : start + PAIRS, :]))
        levels_out(l, core_pairs(*parts), slice(0, PAIRS), own.at[0], up.at[0], down.at[0])


def core_of(kernels, volume):
    counts = (OWN, OWN - 1, OWN - 1)
    return pl.pallas_call(
        core_kernel,
        grid=(4,),
        in_specs=[
            pl.BlockSpec((1, OWN, SIDE, SIDE), lambda i: (jnp.maximum(i - 1, 0), 0, 0, 0)),
            pl.BlockSpec((OWN, SIDE, SIDE), lambda i: (0, 0, 0)),
        ],
        out_specs=[pl.BlockSpec((1, c, PAIRS, SIDE), lambda i: (i, 0, 0, 0)) for c in counts],
        out_shape=[jax.ShapeDtypeStruct((4, c, PAIRS, SIDE), F32) for c in counts],
        name="core",
        compiler_params=ROOM,
        cost_estimate=pl.CostEstimate(flops=1 << 20, bytes_accessed=10 << 20, transcendentals=0),
    )(kernels, volume)


def radial_kernel(below, own, above, out):
    parts = (below, own, above)

    def tile(i, carry):
        at = pl.ds(pl.multiple_of(i * 8, 8), 8)

        def level(j):
            part, k = (0, j) if j < HALF else (1, j - HALF) if j < HALF + OWN else (2, j - HALF - OWN)
            return parts[part][0, k, at, :]

        x = [level(j) for j in range(SPAN)]
        for m in range(OWN):
            c = m + HALF
            total = TAPS[0] * x[c]
            for k in range(1, HALF + 1):
                total = total + TAPS[k] * (x[c - k] + x[c + k])
            out[0, m, at, :] = total
        return carry

    lax.fori_loop(0, out.shape[2] // 8, tile, 0)


def radial(below, own, above):
    count, _, rows, _ = own.shape
    block = rows // 2
    return pl.pallas_call(
        radial_kernel,
        grid=(count, rows // block),
        in_specs=[pl.BlockSpec((1, a.shape[1], block, SIDE), lambda f, i: (f, 0, i, 0)) for a in (below, own, above)],
        out_specs=pl.BlockSpec((1, OWN, block, SIDE), lambda f, i: (f, 0, i, 0)),
        out_shape=jax.ShapeDtypeStruct(own.shape, F32),
        name="radial",
        compiler_params=ROOM,
        cost_estimate=pl.CostEstimate(
            flops=count * OWN * SPAN * rows * SIDE * 2, bytes_accessed=count * 62 * rows * 512, transcendentals=0
        ),
    )(below, own, above)


def pack_kernel(field_count, glued, pair, picks, *refs):
    fields = refs[:field_count]
    out, edge, rows = refs[field_count:]

    def choose(side):
        raw = jnp.where(glued[side] < 2, 1.0, 0.0).astype(F32)
        return picks[side] * raw + picks[side + 2] * (1.0 - raw)

    left_high, left_low = split(jnp.concatenate([choose(0), choose(1)], axis=0))
    left = jnp.concatenate([left_high, left_low], axis=0)
    for f in range(field_count):
        rim = fields[f]
        mine = pl.ds(f * OWN, OWN)
        for q in range(OWN):
            base = q * SIDE
            rows[base : base + DEEP, :] = rim[q, :DEEP, :]
            rows[base + SIDE - DEEP : base + SIDE, :] = rim[q, DEEP : 2 * DEEP, :]
            first, second = unpair(rim[q, 2 * DEEP :, :], None)
            rows[base + DEEP : base + UPPER, :] = first
            rows[base + UPPER : base + SIDE - DEEP, :] = second
        for d in range(DEEP):
            edge[pl.ds(d, OWN, stride=DEEP), :] = rows[pl.ds(d, OWN, stride=SIDE), :]
            edge[pl.ds(OWN * DEEP + d, OWN, stride=DEEP), :] = rows[pl.ds(SIDE - 1 - d, OWN, stride=SIDE), :]
        raw = edge[...]
        across = through(raw, pair[...])
        for side in (2, 3):
            at = slice((side - 2) * OWN * DEEP, (side - 1) * OWN * DEEP)
            strip = jnp.where(glued[side] < 2, raw[at], across[at])
            out[mine, side, :, :] = strip.reshape(OWN, DEEP, SIDE)
        high, low = split(rows[...])
        both = dot_t(left, high)
        strips = both[: 2 * DEEP] + both[2 * DEEP :] + dot_t(left_high, low)
        for q in range(OWN):
            plane = strips[:, q * SIDE : (q + 1) * SIDE]
            out[f * OWN + q, 0, :, :] = plane[:DEEP]
            out[f * OWN + q, 1, :, :] = plane[DEEP:]


def pack(rims, glued, const):
    count = len(rims)
    return pl.pallas_call(
        functools.partial(pack_kernel, count),
        in_specs=[SMEM] + [VMEM] * (2 + count),
        out_specs=VMEM,
        out_shape=jax.ShapeDtypeStruct((count * OWN, 4, DEEP, SIDE), F32),
        scratch_shapes=[pltpu.VMEM((2 * OWN * DEEP, SIDE), F32), pltpu.VMEM((OWN * SIDE, SIDE), F32)],
        name="pack",
        compiler_params=ROOM,
        cost_estimate=pl.CostEstimate(flops=1 << 29, bytes_accessed=6 << 20, transcendentals=0),
    )(glued, const["pair"], const["picks"], *rims)


def route_kernel(source, fix, ends, corner, flipped, strips, out, patch):
    tiles = out.shape[0]
    group = 4

    def move(i, carry):
        for j in range(8):
            e = i * 8 + j
            t, s = i * 2 + j // 4, j % 4
            out[t, s, :, :] = strips[source[e], :, :]
        return carry

    lax.fori_loop(0, tiles // 2, move, 0)
    margins = out[:, 0:2, :, :].reshape(tiles * 2 * DEEP, SIDE)
    high, low = split(margins)
    seen = dot_t(ends[...], high) + dot_t(ends[...], low)
    first, last = seen[:DEEP], seen[DEEP:]
    swap = flipped[...] > 0.5
    turned = jnp.concatenate([jnp.where(swap, last, first), jnp.where(swap, first, last)], axis=0)
    high, low = split(turned)
    for g in range(tiles // group):
        at = slice(g * SIDE, (g + 1) * SIDE)
        added = dot(high[:, at], corner[0]) + dot(high[:, at], corner[1]) + dot(low[:, at], corner[0])
        for j in range(group):
            block = added[:, j * SIDE : (j + 1) * SIDE]
            patch[(g * group + j) * 2] = block[:DEEP]
            patch[(g * group + j) * 2 + 1] = block[DEEP:]
    patch[tiles * 2] = jnp.zeros((DEEP, SIDE), F32)

    def mend(i, carry):
        for j in range(4):
            t, s = i * 2 + j // 2, 2 + j % 2
            out[t, s, :, :] = out[t, s, :, :] + patch[fix[i * 4 + j], :, :]
        return carry

    lax.fori_loop(0, tiles // 2, mend, 0)


def route(strips, tables, const):
    tiles = strips.shape[0]
    source, fix, flipped = tables
    return pl.pallas_call(
        route_kernel,
        in_specs=[SMEM, SMEM] + [VMEM] * 4,
        out_specs=VMEM,
        out_shape=jax.ShapeDtypeStruct((tiles, 4, DEEP, SIDE), F32),
        scratch_shapes=[pltpu.VMEM((tiles * 2 + 1, DEEP, SIDE), F32)],
        name="route",
        compiler_params=ROOM,
        cost_estimate=pl.CostEstimate(flops=1 << 28, bytes_accessed=4 << 20, transcendentals=0),
    )(source, fix, const["ends"], const["corner"], flipped, strips.reshape(tiles * 4, DEEP, SIDE))


def base_kernel(glued, pair, along, core, *refs):
    rims = refs[:4]
    out, rows, across = refs[4:]
    f = pl.program_id(0)
    lane = lanes((SIDE, along.shape[1]))
    south = jnp.where(glued[2] < 2, 1.0, 0.0).astype(F32)
    north = jnp.where(glued[3] < 2, 1.0, 0.0).astype(F32)
    scale = jnp.where(lane < SIDE, 1.0, jnp.where(lane < SIDE + DEEP, south, north))
    left_high, left_low = split(along[...] * scale)
    left = jnp.concatenate([left_high, left_low], axis=0)
    for k in range(4):

        @pl.when(f == k)
        def _():
            for q in range(OWN):
                base = q * SIDE
                rows[base : base + DEEP, :] = rims[k][q, :DEEP, :]
                rows[base + SIDE - DEEP : base + SIDE, :] = rims[k][q, DEEP : 2 * DEEP, :]
                first, second = unpair(rims[k][q, 2 * DEEP :, :], core[0, q])
                rows[base + DEEP : base + UPPER, :] = first
                rows[base + UPPER : base + SIDE - DEEP, :] = second

    across[...] = through(rows[...], pair[...])

    def column(q):
        base = q * SIDE
        own = [rows[base : base + DEEP, :], rows[base + SIDE - DEEP : base + SIDE, :]]
        return jnp.concatenate([across[base : base + SIDE, :]] + own, axis=0)

    for q in range(0, OWN, 2):
        high, low = split(jnp.concatenate([column(q), column(q + 1)], axis=1))
        both = dot(left, high)
        total = both[:SIDE] + both[SIDE:] + dot(left_high, low)
        out[0, q] = total[:, :SIDE]
        out[0, q + 1] = total[:, SIDE:]


def base_lateral(rims, core, glued, const):
    plane = (1, OWN, SIDE, SIDE)
    return pl.pallas_call(
        base_kernel,
        grid=(4,),
        in_specs=[
            SMEM,
            pl.BlockSpec(const["pair"].shape, lambda i: (0, 0)),
            pl.BlockSpec(const["along"].shape, lambda i: (0, 0)),
            pl.BlockSpec((1, OWN, PAIRS, SIDE), lambda i: (i, 0, 0, 0)),
        ]
        + [pl.BlockSpec((OWN, RIM, SIDE), lambda i: (0, 0, 0))] * 4,
        out_specs=pl.BlockSpec(plane, lambda i: (i, 0, 0, 0)),
        out_shape=jax.ShapeDtypeStruct((4,) + plane[1:], F32),
        scratch_shapes=[pltpu.VMEM((OWN * SIDE, SIDE), F32)] * 2,
        name="base",
        compiler_params=ROOM,
        cost_estimate=pl.CostEstimate(flops=1 << 32, bytes_accessed=9 << 20, transcendentals=0),
    )(glued, const["pair"], const["along"], core, *rims)


def turn(code):
    row = lax.broadcasted_iota(jnp.int32, (SIDE, SIDE), 0)
    col = lax.broadcasted_iota(jnp.int32, (SIDE, SIDE), 1)
    return jnp.where(col == jnp.where(code == 1, SIDE - 1 - row, row), 1.0, 0.0).astype(BF16)


def finish_kernel(turned, square, ahead, spread, margins, base, out, below, ways):
    f = pl.program_id(0)
    size = OWN * DEEP

    @pl.when(f == 0)
    def _():
        for side in range(4):
            way = turn(turned[side])
            if side < 2:
                ways[side, 0] = dot(square[0], way).astype(BF16)
                ways[side, 1] = dot(square[1], way).astype(BF16)
            else:
                ways[side, 0] = way

    def margin(side):
        return split(margins[:, side, :, :].reshape(size, SIDE))

    sides = []
    for side in (0, 1):
        high, low = margin(side)
        both = dot_t(ways[side].reshape(2 * SIDE, SIDE), high)
        sides.append(both[:SIDE] + both[SIDE:] + dot_t(ways[side, 0], low))
    rows = []
    for side in (2, 3):
        high, low = margin(side)
        way = ways[side, 0]
        rows.append((dot(high, way) + dot(low, way)).reshape(OWN, DEEP, SIDE))
    planes = 4
    for g in range(OWN // planes):
        at = slice(g * planes * DEEP, (g + 1) * planes * DEEP)
        high, low = split(jnp.concatenate([sides[0][:, at], sides[1][:, at]], axis=1))
        left = jnp.concatenate([high, low], axis=1)
        for j in range(0, planes, 2):
            to = slice(j * SIDE, (j + 2) * SIDE)
            total = dot(left, spread[: 2 * SIDE, to]) + dot(high, spread[2 * SIDE :, to])
            q = g * planes + j
            pairs = [jnp.concatenate([rows[0][k], rows[1][k]], axis=0) for k in (q, q + 1)]
            right, rest = split(jnp.concatenate(pairs, axis=1))
            total = total + dot(ahead[...], jnp.concatenate([right, rest, right], axis=0))
            for k in range(2):
                plane = total[:, k * SIDE : (k + 1) * SIDE] + base[0, q + k]

                @pl.when(f == 0)
                def _():
                    below[q + k] = 1.0 / plane

                @pl.when(f > 0)
                def _():
                    out[0, q + k] = plane * below[q + k]


def finish(base, margins, turned, const):
    plane = (1, OWN, SIDE, SIDE)
    return pl.pallas_call(
        finish_kernel,
        grid=(4,),
        in_specs=[
            SMEM,
            pl.BlockSpec(const["square"].shape, lambda i: (0, 0, 0)),
            pl.BlockSpec(const["ahead"].shape, lambda i: (0, 0)),
            pl.BlockSpec(const["spread"].shape, lambda i: (0, 0)),
            pl.BlockSpec((OWN, 4, DEEP, SIDE), lambda i: (i, 0, 0, 0)),
            pl.BlockSpec(plane, lambda i: (i, 0, 0, 0)),
        ],
        out_specs=pl.BlockSpec(plane, lambda i: (jnp.maximum(i - 1, 0), 0, 0, 0)),
        out_shape=jax.ShapeDtypeStruct((3,) + plane[1:], F32),
        scratch_shapes=[pltpu.VMEM(plane[1:], F32), pltpu.VMEM((4, 2, SIDE, SIDE), BF16)],
        name="finish",
        compiler_params=ROOM,
        cost_estimate=pl.CostEstimate(flops=1 << 32, bytes_accessed=9 << 20, transcendentals=0),
    )(turned, const["square"], const["ahead"], const["spread"], margins, base)


UP = [(0, 1), (1, 2), (2, 3)]
DOWN = [(1, 0), (2, 1), (3, 2)]


def with_halo(own, up, down):
    return lax.ppermute(up, "slab", UP), own, lax.ppermute(down, "slab", DOWN)


def per_device(kernels, volume, neighbours, glued_sides, reversals):
    const = {k: jnp.asarray(v) for k, v in constants().items()}
    tile = lax.axis_index("tile")
    glued = glued_sides[tile]
    turned = reversals[tile]
    tiles = neighbours.shape[0]
    source = (neighbours * 4 + glued_sides).reshape(-1)
    ahead = glued_sides[:, 2:]
    fix = jnp.where(ahead >= 2, neighbours[:, 2:] * 2 + ahead - 2, tiles * 2).reshape(-1)
    flipped = jnp.repeat(reversals[:, :2].astype(F32).reshape(-1), DEEP)[None, :]
    tables = (source, fix, flipped)

    def to_all(x):
        return lax.all_to_all(x, "tile", split_axis=0, concat_axis=0, tiled=True)

    rims = []
    for f in (None, 0, 1, 2):
        parts = rim_of(kernels[0], volume, f)
        rims.append(radial(*[x[None] for x in with_halo(*parts)])[0])
    own, up, down = core_of(kernels[0], volume[0])
    below, own, above = with_halo(own, up, down)
    routed_in = to_all(pack(rims, glued, const))
    routed = route(routed_in, tables, const)
    margins = to_all(routed)
    base = base_lateral(rims, radial(below, own, above), glued, const)
    return finish(base, margins, turned, const)[None]


def solution(mesh):
    placed = (P("tile", None, "slab", None, None), P("tile", "slab", None, None), P(), P(), P())
    return jax.shard_map(
        per_device,
        mesh=mesh,
        in_specs=placed,
        out_specs=P("tile", None, "slab", None, None),
        check_vma=False,
    )
```

```python
import functools
import math

import jax
import jax.numpy as jnp
import numpy as np
from jax import lax
from jax.experimental import pallas as pl
from jax.experimental.pallas import tpu as pltpu
from jax.sharding import PartitionSpec as P


SIDE = 128
HALF = 15
DEEP = 16
OWN = 16
SPAN = 2 * HALF + OWN
F32 = jnp.float32
BF16 = jnp.bfloat16

ROOM = pltpu.CompilerParams(vmem_limit_bytes=24 << 20)
TAPS = [float(np.float32(math.exp(-k * k / 50.0))) for k in range(HALF + 1)]


def tap(offset):
    offset = np.abs(np.asarray(offset))
    return np.where(offset <= HALF, np.exp(-(offset.astype(np.float64) ** 2) / 50.0), 0.0).astype(np.float32)


def halves(values):
    high = values.astype(BF16)
    low = (values - high.astype(np.float32)).astype(BF16)
    return high, low


def constants():
    cell = np.arange(SIDE)
    deep = np.arange(DEEP)
    live = (deep < HALF)[:, None]
    square = tap(cell[:, None] - cell[None, :])
    high, low = halves(square)
    pair = np.block([[high, low], [high, np.zeros_like(low)]])
    near = tap(cell[None, :] + deep[:, None] + 1) * live
    far = tap(SIDE - cell[None, :] + deep[:, None]) * live
    pick_west = (cell[None, :] == deep[:, None]).astype(np.float32) * live
    pick_east = (cell[None, :] == SIDE - 1 - deep[:, None]).astype(np.float32) * live
    sum_west = tap(cell[None, :] - deep[:, None]) * live
    sum_east = tap(cell[None, :] - (SIDE - 1 - deep[:, None])) * live
    picks = np.stack([pick_west, pick_east, sum_west, sum_east])
    back = tap(deep[:, None] + deep[None, :] + 1) * live * live.T
    south_own = near.T.astype(np.float64) @ back
    north_own = (far.T.astype(np.float64) @ back)[:, ::-1]
    along = np.concatenate([square, south_own, north_own], axis=1).astype(np.float32)
    ahead_high, ahead_low = halves(np.concatenate([near.T, far.T], axis=1))
    eye = np.eye(4, dtype=np.float32)
    spread_high, spread_low = halves(np.concatenate([np.kron(eye, near), np.kron(eye, far)], axis=0))
    corner_high, corner_low = halves(np.kron(eye, np.concatenate([near, far], axis=0)))
    ends = np.concatenate([pick_west, pick_east], axis=0)
    return dict(
        pair=pair,
        picks=picks,
        along=along,
        square=np.stack([high, low]),
        ahead=np.concatenate([ahead_high, ahead_high, ahead_low], axis=1),
        spread=np.concatenate([spread_high, spread_high, spread_low], axis=0),
        corner=np.concatenate([corner_high, corner_high, corner_low], axis=0),
        ends=ends.astype(BF16),
    )


def split(values):
    high = values.astype(BF16)
    return high, (values - high.astype(F32)).astype(BF16)


def dot(left, right):
    return jnp.dot(left, right, preferred_element_type=F32)


def dot_t(left, right):
    return lax.dot_general(left, right, (((1,), (1,)), ((), ())), preferred_element_type=F32)


def through(rows, pair):
    high, low = split(rows)
    both = dot(jnp.concatenate([high, low], axis=1), pair)
    return both[:, :SIDE] + both[:, SIDE:]


VMEM = pl.BlockSpec(memory_space=pltpu.VMEM)
SMEM = pl.BlockSpec(memory_space=pltpu.SMEM)


PAIRS = 48
RIM = 2 * DEEP + PAIRS
QUARTER = SIDE // 4
UPPER = DEEP + PAIRS


def lanes(shape):
    return lax.broadcasted_iota(jnp.int32, shape, len(shape) - 1)


def rolled(x, amount):
    return pltpu.roll(x, amount, x.ndim - 1)


def two(first, second):
    return jnp.where(lanes(first.shape) < SIDE // 2, first, second)


def rim_pairs(first, second):
    return two(rolled(first, QUARTER), rolled(second, 3 * QUARTER))


def core_pairs(first, second):
    return two(rolled(first, 3 * QUARTER), rolled(second, QUARTER))


def unpair(rim, core):
    edge = lanes(rim.shape)
    edge = (edge < QUARTER) | (edge >= 3 * QUARTER)
    inside = (rolled(core, QUARTER), rolled(core, 3 * QUARTER)) if core is not None else (0.0, 0.0)
    return jnp.where(edge, rolled(rim, 3 * QUARTER), inside[0]), jnp.where(edge, rolled(rim, QUARTER), inside[1])


def levels_out(l, value, at, own, up, down):
    own[l, at, :] = value
    if l > 0:
        up[l - 1, at, :] = value
    if l < OWN - 1:
        down[l, at, :] = value


def levels_of(first, kernels, volume):
    def rows(l, start, count):
        w = volume[0, l, start : start + count, :]
        product = w * kernels[0, l, start : start + count, :]
        if first is None:
            return product
        field = jnp.full(w.shape, pl.program_id(0), jnp.int32)
        return jnp.where(field == first, w, product)

    return rows


def rim_kernel(first, kernels, volume, own, up, down):
    outs = own.at[0], up.at[0], down.at[0]
    rows = levels_of(first, kernels, volume)
    for l in range(OWN):
        levels_out(l, rows(l, 0, DEEP), slice(0, DEEP), *outs)
        levels_out(l, rows(l, SIDE - DEEP, DEEP), slice(DEEP, 2 * DEEP), *outs)
        levels_out(l, rim_pairs(rows(l, DEEP, PAIRS), rows(l, UPPER, PAIRS)), slice(2 * DEEP, RIM), *outs)


def core_kernel(first, kernels, volume, own, up, down):
    outs = own.at[0], up.at[0], down.at[0]
    rows = levels_of(first, kernels, volume)
    for l in range(OWN):
        levels_out(l, core_pairs(rows(l, DEEP, PAIRS), rows(l, UPPER, PAIRS)), slice(0, PAIRS), *outs)


def part_of(kernel, rows, kernels, volume, fields):
    start, count = fields[0], len(fields)
    counts = (OWN, OWN - 1, OWN - 1)
    return pl.pallas_call(
        functools.partial(kernel, 0 if start == 0 else None),
        grid=(count,),
        in_specs=[
            pl.BlockSpec((1, OWN, SIDE, SIDE), lambda i: (jnp.maximum(i + start - 1, 0), 0, 0, 0)),
            pl.BlockSpec((1, OWN, SIDE, SIDE), lambda i: (0, 0, 0, 0)),
        ],
        out_specs=[pl.BlockSpec((1, c, rows, SIDE), lambda i: (i, 0, 0, 0)) for c in counts],
        out_shape=[jax.ShapeDtypeStruct((count, c, rows, SIDE), F32) for c in counts],
        name="part",
        compiler_params=ROOM,
        cost_estimate=pl.CostEstimate(flops=1 << 20, bytes_accessed=count * 3 << 20, transcendentals=0),
    )(kernels, volume)


def radial_rows(below, own, above, out):
    parts = (below, own, above)

    def tile(i, carry):
        at = pl.ds(pl.multiple_of(i * 8, 8), 8)

        def level(j):
            part, k = (0, j) if j < HALF else (1, j - HALF) if j < HALF + OWN else (2, j - HALF - OWN)
            return parts[part][k, at, :]

        x = [level(j) for j in range(SPAN)]
        for m in range(OWN):
            c = m + HALF
            total = TAPS[0] * x[c]
            for k in range(1, HALF + 1):
                total = total + TAPS[k] * (x[c - k] + x[c + k])
            out[m, at, :] = total
        return carry

    lax.fori_loop(0, out.shape[1] // 8, tile, 0)


def radial_kernel(*refs):
    radial_rows(*[r.at[0] for r in refs])


def radial(below, own, above):
    count, _, rows, _ = own.shape
    block = rows // 2
    return pl.pallas_call(
        radial_kernel,
        grid=(count, rows // block),
        in_specs=[pl.BlockSpec((1, a.shape[1], block, SIDE), lambda f, i: (f, 0, i, 0)) for a in (below, own, above)],
        out_specs=pl.BlockSpec((1, OWN, block, SIDE), lambda f, i: (f, 0, i, 0)),
        out_shape=jax.ShapeDtypeStruct(own.shape, F32),
        name="radial",
        compiler_params=ROOM,
        cost_estimate=pl.CostEstimate(
            flops=count * OWN * SPAN * rows * SIDE * 2, bytes_accessed=count * 62 * rows * 512, transcendentals=0
        ),
    )(below, own, above)


def strips_kernel(glued, pair, picks, below, own, above, *refs):
    out, rim, edge, rows = refs[-4:]

    def choose(side):
        raw = jnp.where(glued[side] < 2, 1.0, 0.0).astype(F32)
        return picks[side] * raw + picks[side + 2] * (1.0 - raw)

    radial_rows(below.at[0], own.at[0], above.at[0], rim)
    left_high, left_low = split(jnp.concatenate([choose(0), choose(1)], axis=0))
    left = jnp.concatenate([left_high, left_low], axis=0)
    for q in range(OWN):
        base = q * SIDE
        rows[base : base + DEEP, :] = rim[q, :DEEP, :]
        rows[base + SIDE - DEEP : base + SIDE, :] = rim[q, DEEP : 2 * DEEP, :]
        first, second = unpair(rim[q, 2 * DEEP :, :], None)
        rows[base + DEEP : base + UPPER, :] = first
        rows[base + UPPER : base + SIDE - DEEP, :] = second
    for d in range(DEEP):
        edge[pl.ds(d, OWN, stride=DEEP), :] = rows[pl.ds(d, OWN, stride=SIDE), :]
        edge[pl.ds(OWN * DEEP + d, OWN, stride=DEEP), :] = rows[pl.ds(SIDE - 1 - d, OWN, stride=SIDE), :]
    raw = edge[...]
    across = through(raw, pair[...])
    for side in (2, 3):
        at = slice((side - 2) * OWN * DEEP, (side - 1) * OWN * DEEP)
        strip = jnp.where(glued[side] < 2, raw[at], across[at])
        out[:, side, :, :] = strip.reshape(OWN, DEEP, SIDE)
    high, low = split(rows[...])
    both = dot_t(left, high)
    strips = both[: 2 * DEEP] + both[2 * DEEP :] + dot_t(left_high, low)
    for q in range(OWN):
        plane = strips[:, q * SIDE : (q + 1) * SIDE]
        out[q, 0, :, :] = plane[:DEEP]
        out[q, 1, :, :] = plane[DEEP:]


def add_strips(strips, field, halo, place, glued, const):
    arrays = [glued, const["pair"], const["picks"], *halo]
    specs = [SMEM] + [pl.BlockSpec(a.shape, lambda i, n=a.ndim: (0,) * n) for a in arrays[1:3]]
    specs += [pl.BlockSpec((1,) + a.shape[1:], lambda i: (place, 0, 0, 0)) for a in halo]
    aliases = {}
    if strips is not None:
        aliases = {len(arrays): 0}
        arrays.append(strips)
        specs.append(pl.BlockSpec(memory_space=pl.ANY))
    return pl.pallas_call(
        strips_kernel,
        grid=(1,),
        in_specs=specs,
        out_specs=[
            pl.BlockSpec((OWN, 4, DEEP, SIDE), lambda i: (field, 0, 0, 0)),
            pl.BlockSpec((OWN, RIM, SIDE), lambda i: (0, 0, 0)),
        ],
        out_shape=[
            jax.ShapeDtypeStruct((4 * OWN, 4, DEEP, SIDE), F32),
            jax.ShapeDtypeStruct((OWN, RIM, SIDE), F32),
        ],
        scratch_shapes=[pltpu.VMEM((2 * OWN * DEEP, SIDE), F32), pltpu.VMEM((OWN * SIDE, SIDE), F32)],
        input_output_aliases=aliases,
        name="strips",
        compiler_params=ROOM,
        cost_estimate=pl.CostEstimate(flops=1 << 27, bytes_accessed=3 << 20, transcendentals=0),
    )(*arrays)


def route_kernel(source, fix, ends, corner, flipped, strips, out, patch):
    tiles = out.shape[0]
    group = 4

    def move(i, carry):
        for j in range(8):
            t, s = i * 4 + j // 2, j % 2
            out[t, s, :, :] = strips[source[t * 4 + s], :, :]
        return carry

    lax.fori_loop(0, tiles // 4, move, 0)
    margins = out[:, 0:2, :, :].reshape(tiles * 2 * DEEP, SIDE)
    high, low = split(margins)
    seen = dot_t(ends[...], high) + dot_t(ends[...], low)
    first, last = seen[:DEEP], seen[DEEP:]
    swap = flipped[...] > 0.5
    turned = jnp.concatenate([jnp.where(swap, last, first), jnp.where(swap, first, last)], axis=0)
    groups = tiles // group
    high, low = [
        jnp.concatenate([x[:, g * SIDE : (g + 1) * SIDE] for g in range(groups)], axis=0) for x in split(turned)
    ]
    added = dot(jnp.concatenate([high, low], axis=1), corner[: 2 * SIDE]) + dot(high, corner[2 * SIDE :])
    for g in range(groups):
        for j in range(group):
            block = added[g * 2 * DEEP : (g + 1) * 2 * DEEP, j * SIDE : (j + 1) * SIDE]
            patch[(g * group + j) * 2] = block[:DEEP]
            patch[(g * group + j) * 2 + 1] = block[DEEP:]
    patch[tiles * 2] = jnp.zeros((DEEP, SIDE), F32)

    def mend(i, carry):
        for j in range(8):
            t, s = i * 4 + j // 2, j % 2
            out[t, 2 + s, :, :] = strips[source[t * 4 + 2 + s], :, :] + patch[fix[t * 2 + s], :, :]
        return carry

    lax.fori_loop(0, tiles // 4, mend, 0)


def route(strips, tables, const):
    tiles = strips.shape[0]
    source, fix, flipped = tables
    return pl.pallas_call(
        route_kernel,
        in_specs=[SMEM, SMEM] + [VMEM] * 4,
        out_specs=VMEM,
        out_shape=jax.ShapeDtypeStruct((tiles, 4, DEEP, SIDE), F32),
        scratch_shapes=[pltpu.VMEM((tiles * 2 + 1, DEEP, SIDE), F32)],
        name="route",
        compiler_params=ROOM,
        cost_estimate=pl.CostEstimate(flops=1 << 28, bytes_accessed=4 << 20, transcendentals=0),
    )(source, fix, const["ends"], const["corner"], flipped, strips.reshape(tiles * 4, DEEP, SIDE))


def base_kernel(glued, pair, along, *refs):
    cores, rims = refs[:2], refs[2:6]
    out, rows, across = refs[6:]
    f = pl.program_id(0)
    lane = lanes((SIDE, along.shape[1]))
    south = jnp.where(glued[2] < 2, 1.0, 0.0).astype(F32)
    north = jnp.where(glued[3] < 2, 1.0, 0.0).astype(F32)
    scale = jnp.where(lane < SIDE, 1.0, jnp.where(lane < SIDE + DEEP, south, north))
    left_high, left_low = split(along[...] * scale)
    left = jnp.concatenate([left_high, left_low], axis=0)
    for k in range(4):

        @pl.when(f == k)
        def _():
            for q in range(OWN):
                base = q * SIDE
                rows[base : base + DEEP, :] = rims[k][q, :DEEP, :]
                rows[base + SIDE - DEEP : base + SIDE, :] = rims[k][q, DEEP : 2 * DEEP, :]
                first, second = unpair(rims[k][q, 2 * DEEP :, :], cores[min(k, 1)][0, q])
                rows[base + DEEP : base + UPPER, :] = first
                rows[base + UPPER : base + SIDE - DEEP, :] = second

    across[...] = through(rows[...], pair[...])

    def column(q):
        base = q * SIDE
        own = [rows[base : base + DEEP, :], rows[base + SIDE - DEEP : base + SIDE, :]]
        return jnp.concatenate([across[base : base + SIDE, :]] + own, axis=0)

    for q in range(0, OWN, 2):
        high, low = split(jnp.concatenate([column(q), column(q + 1)], axis=1))
        both = dot(left, high)
        total = both[:SIDE] + both[SIDE:] + dot(left_high, low)
        out[0, q] = total[:, :SIDE]
        out[0, q + 1] = total[:, SIDE:]


def base_lateral(rims, cores, glued, const):
    plane = (1, OWN, SIDE, SIDE)
    return pl.pallas_call(
        base_kernel,
        grid=(4,),
        in_specs=[
            SMEM,
            pl.BlockSpec(const["pair"].shape, lambda i: (0, 0)),
            pl.BlockSpec(const["along"].shape, lambda i: (0, 0)),
            pl.BlockSpec((1, OWN, PAIRS, SIDE), lambda i: (0, 0, 0, 0)),
            pl.BlockSpec((1, OWN, PAIRS, SIDE), lambda i: (jnp.maximum(i - 1, 0), 0, 0, 0)),
        ]
        + [pl.BlockSpec((OWN, RIM, SIDE), lambda i: (0, 0, 0))] * 4,
        out_specs=pl.BlockSpec(plane, lambda i: (i, 0, 0, 0)),
        out_shape=jax.ShapeDtypeStruct((4,) + plane[1:], F32),
        scratch_shapes=[pltpu.VMEM((OWN * SIDE, SIDE), F32)] * 2,
        name="base",
        compiler_params=ROOM,
        cost_estimate=pl.CostEstimate(flops=1 << 32, bytes_accessed=9 << 20, transcendentals=0),
    )(glued, const["pair"], const["along"], *cores, *rims)


def turn(code):
    row = lax.broadcasted_iota(jnp.int32, (SIDE, SIDE), 0)
    col = lax.broadcasted_iota(jnp.int32, (SIDE, SIDE), 1)
    return jnp.where(col == jnp.where(code == 1, SIDE - 1 - row, row), 1.0, 0.0).astype(BF16)


def finish_kernel(turned, square, ahead, spread, margins, base, out, below, ways):
    f = pl.program_id(0)
    size = OWN * DEEP

    @pl.when(f == 0)
    def _():
        for side in range(4):
            way = turn(turned[side])
            if side < 2:
                ways[side, 0] = dot(square[0], way).astype(BF16)
                ways[side, 1] = dot(square[1], way).astype(BF16)
            else:
                ways[side, 0] = way

    def margin(side):
        return split(margins[:, side, :, :].reshape(size, SIDE))

    def planes_of(emit):
        sides = []
        for side in (0, 1):
            high, low = margin(side)
            both = dot_t(ways[side].reshape(2 * SIDE, SIDE), high)
            sides.append(both[:SIDE] + both[SIDE:] + dot_t(ways[side, 0], low))
        rows = []
        for side in (2, 3):
            high, low = margin(side)
            way = ways[side, 0]
            rows.append((dot(high, way) + dot(low, way)).reshape(OWN, DEEP, SIDE))
        planes, groups = 4, 4
        parts = []
        for g in range(groups):
            at = slice(g * planes * DEEP, (g + 1) * planes * DEEP)
            parts.append(split(jnp.concatenate([sides[0][:, at], sides[1][:, at]], axis=1)))
        high = jnp.concatenate([x for x, _ in parts], axis=0)
        left = jnp.concatenate([high, jnp.concatenate([x for _, x in parts], axis=0)], axis=1)
        for j in range(0, planes, 2):
            to = slice(j * SIDE, (j + 2) * SIDE)
            added = dot(left, spread[: 2 * SIDE, to])
            for g in range(groups):
                q = g * planes + j
                pairs = [jnp.concatenate([rows[0][k], rows[1][k]], axis=0) for k in (q, q + 1)]
                right, rest = split(jnp.concatenate(pairs, axis=1))
                last = jnp.concatenate([parts[g][0], ahead[...]], axis=1)
                total = added[g * SIDE : (g + 1) * SIDE] + dot(
                    last, jnp.concatenate([spread[2 * SIDE :, to], right, rest, right], axis=0)
                )
                for k in range(2):
                    emit(q + k, total[:, k * SIDE : (k + 1) * SIDE] + base[0, q + k])

    @pl.when(f == 0)
    def _():
        def keep(q, plane):
            below[q] = 1.0 / plane

        planes_of(keep)

    @pl.when(f > 0)
    def _():
        def divide(q, plane):
            out[0, q] = plane * below[q]

        planes_of(divide)


def finish(base, margins, turned, const):
    plane = (1, OWN, SIDE, SIDE)
    return pl.pallas_call(
        finish_kernel,
        grid=(4,),
        in_specs=[
            SMEM,
            pl.BlockSpec(const["square"].shape, lambda i: (0, 0, 0)),
            pl.BlockSpec(const["ahead"].shape, lambda i: (0, 0)),
            pl.BlockSpec(const["spread"].shape, lambda i: (0, 0)),
            pl.BlockSpec((OWN, 4, DEEP, SIDE), lambda i: (i, 0, 0, 0)),
            pl.BlockSpec(plane, lambda i: (i, 0, 0, 0)),
        ],
        out_specs=pl.BlockSpec(plane, lambda i: (jnp.maximum(i - 1, 0), 0, 0, 0)),
        out_shape=jax.ShapeDtypeStruct((3,) + plane[1:], F32),
        scratch_shapes=[pltpu.VMEM(plane[1:], F32), pltpu.VMEM((4, 2, SIDE, SIDE), BF16)],
        name="finish",
        compiler_params=ROOM,
        cost_estimate=pl.CostEstimate(flops=1 << 32, bytes_accessed=9 << 20, transcendentals=0),
    )(turned, const["square"], const["ahead"], const["spread"], margins, base)


UP = [(0, 1), (1, 2), (2, 3)]
DOWN = [(1, 0), (2, 1), (3, 2)]


def with_halo(own, up, down):
    return lax.ppermute(up, "slab", UP), own, lax.ppermute(down, "slab", DOWN)


def per_device(kernels, volume, neighbours, glued_sides, reversals):
    const = {k: jnp.asarray(v) for k, v in constants().items()}
    tile = lax.axis_index("tile")
    glued = glued_sides[tile]
    turned = reversals[tile]
    tiles = neighbours.shape[0]
    source = (neighbours * 4 + glued_sides).reshape(-1)
    ahead = glued_sides[:, 2:]
    fix = jnp.where(ahead >= 2, neighbours[:, 2:] * 2 + ahead - 2, tiles * 2).reshape(-1)
    flipped = jnp.repeat(reversals[:, :2].astype(F32).reshape(-1), DEEP)[None, :]
    tables = (source, fix, flipped)

    def to_all(x):
        return lax.all_to_all(x, "tile", split_axis=0, concat_axis=0, tiled=True)

    def in_hbm(x):
        return pltpu.with_memory_space_constraint(x, pltpu.HBM)

    source_kernels, source_volume = in_hbm(kernels[0]), in_hbm(volume)
    rims, strips = [], None
    for fields in ((0,), (1, 2), (3,)):
        parts = part_of(rim_kernel, RIM, source_kernels, source_volume, fields)
        halo = with_halo(*parts)
        for place, f in enumerate(fields):
            strips, rim = add_strips(strips, f, halo, place, glued, const)
            rims.append(in_hbm(rim))
    cores = []
    for fields in ((0,), (1, 2, 3)):
        parts = part_of(core_kernel, PAIRS, source_kernels, source_volume, fields)
        cores.append(with_halo(*parts))
    routed_in = to_all(strips)
    routed = route(routed_in, tables, const)
    margins = to_all(routed)
    base = in_hbm(base_lateral(rims, [radial(*x) for x in cores], glued, const))
    return finish(base, margins, turned, const)[None]


def solution(mesh):
    placed = (P("tile", None, "slab", None, None), P("tile", "slab", None, None), P(), P(), P())
    return jax.shard_map(
        per_device,
        mesh=mesh,
        in_specs=placed,
        out_specs=P("tile", None, "slab", None, None),
        check_vma=False,
    )
```

```python
import functools
import math

import jax
import jax.numpy as jnp
import numpy as np
from jax import lax
from jax.experimental import pallas as pl
from jax.experimental.pallas import tpu as pltpu
from jax.sharding import PartitionSpec as P


SIDE = 128
HALF = 15
DEEP = 16
OWN = 16
SPAN = 2 * HALF + OWN
F32 = jnp.float32
BF16 = jnp.bfloat16

ROOM = pltpu.CompilerParams(vmem_limit_bytes=24 << 20)
TAPS = [float(np.float32(math.exp(-k * k / 50.0))) for k in range(HALF + 1)]


def tap(offset):
    offset = np.abs(np.asarray(offset))
    return np.where(offset <= HALF, np.exp(-(offset.astype(np.float64) ** 2) / 50.0), 0.0).astype(np.float32)


def halves(values):
    high = values.astype(BF16)
    low = (values - high.astype(np.float32)).astype(BF16)
    return high, low


def constants():
    cell = np.arange(SIDE)
    deep = np.arange(DEEP)
    live = (deep < HALF)[:, None]
    square = tap(cell[:, None] - cell[None, :])
    high, low = halves(square)
    pair = np.block([[high, low], [high, np.zeros_like(low)]])
    near = tap(cell[None, :] + deep[:, None] + 1) * live
    far = tap(SIDE - cell[None, :] + deep[:, None]) * live
    pick_west = (cell[None, :] == deep[:, None]).astype(np.float32) * live
    pick_east = (cell[None, :] == SIDE - 1 - deep[:, None]).astype(np.float32) * live
    sum_west = tap(cell[None, :] - deep[:, None]) * live
    sum_east = tap(cell[None, :] - (SIDE - 1 - deep[:, None])) * live
    picks = np.stack([pick_west, pick_east, sum_west, sum_east])
    back = tap(deep[:, None] + deep[None, :] + 1) * live * live.T
    south_own = near.T.astype(np.float64) @ back
    north_own = (far.T.astype(np.float64) @ back)[:, ::-1]
    along = np.concatenate([square, south_own, north_own], axis=1).astype(np.float32)
    ahead_high, ahead_low = halves(np.concatenate([near.T, far.T], axis=1))
    eye = np.eye(4, dtype=np.float32)
    spread_high, spread_low = halves(np.concatenate([np.kron(eye, near), np.kron(eye, far)], axis=0))
    corner_high, corner_low = halves(np.kron(eye, np.concatenate([near, far], axis=0)))
    ends = np.concatenate([pick_west, pick_east], axis=0)
    return dict(
        pair=pair,
        picks=picks,
        along=along,
        square=np.stack([high, low]),
        ahead=np.concatenate([ahead_high, ahead_high, ahead_low], axis=1),
        spread=np.concatenate([spread_high, spread_high, spread_low], axis=0),
        corner=np.concatenate([corner_high, corner_high, corner_low], axis=0),
        ends=ends.astype(BF16),
    )


def split(values):
    high = values.astype(BF16)
    return high, (values - high.astype(F32)).astype(BF16)


def dot(left, right):
    return jnp.dot(left, right, preferred_element_type=F32)


def dot_t(left, right):
    return lax.dot_general(left, right, (((1,), (1,)), ((), ())), preferred_element_type=F32)


def through(rows, pair):
    high, low = split(rows)
    both = dot(jnp.concatenate([high, low], axis=1), pair)
    return both[:, :SIDE] + both[:, SIDE:]


VMEM = pl.BlockSpec(memory_space=pltpu.VMEM)
SMEM = pl.BlockSpec(memory_space=pltpu.SMEM)


PAIRS = 48
RIM = 2 * DEEP + PAIRS
QUARTER = SIDE // 4
UPPER = DEEP + PAIRS


def lanes(shape):
    return lax.broadcasted_iota(jnp.int32, shape, len(shape) - 1)


def rolled(x, amount):
    return pltpu.roll(x, amount, x.ndim - 1)


def two(first, second):
    return jnp.where(lanes(first.shape) < SIDE // 2, first, second)


def rim_pairs(first, second):
    return two(rolled(first, QUARTER), rolled(second, 3 * QUARTER))


def core_pairs(first, second):
    return two(rolled(first, 3 * QUARTER), rolled(second, QUARTER))


def unpair(rim, core):
    edge = lanes(rim.shape)
    edge = (edge < QUARTER) | (edge >= 3 * QUARTER)
    inside = (rolled(core, QUARTER), rolled(core, 3 * QUARTER)) if core is not None else (0.0, 0.0)
    return jnp.where(edge, rolled(rim, 3 * QUARTER), inside[0]), jnp.where(edge, rolled(rim, QUARTER), inside[1])


def halo_out(odd, own, near, cross):
    def level(j, carry):
        near[j, :, :] = own[j + 1 - odd[0], :, :]
        cross[j, :, :] = own[j + odd[0], :, :]
        return carry

    lax.fori_loop(0, OWN - 1, level, 0)


def levels_of(first, kernels, volume):
    def rows(l, start, count):
        w = volume[0, l, start : start + count, :]
        product = w * kernels[0, l, start : start + count, :]
        if first is None:
            return product
        field = jnp.full(w.shape, pl.program_id(0), jnp.int32)
        return jnp.where(field == first, w, product)

    return rows


def rim_kernel(first, odd, kernels, volume, own, near, cross):
    rows = levels_of(first, kernels, volume)
    for l in range(OWN):
        own[0, l, :DEEP, :] = rows(l, 0, DEEP)
        own[0, l, DEEP : 2 * DEEP, :] = rows(l, SIDE - DEEP, DEEP)
        own[0, l, 2 * DEEP :, :] = rim_pairs(rows(l, DEEP, PAIRS), rows(l, UPPER, PAIRS))
    halo_out(odd, own.at[0], near.at[0], cross.at[0])


def core_kernel(first, odd, kernels, volume, own, near, cross):
    rows = levels_of(first, kernels, volume)
    for l in range(OWN):
        own[0, l] = core_pairs(rows(l, DEEP, PAIRS), rows(l, UPPER, PAIRS))
    halo_out(odd, own.at[0], near.at[0], cross.at[0])


def part_of(kernel, rows, odd, kernels, volume, fields):
    start, count = fields[0], len(fields)
    counts = (OWN, OWN - 1, OWN - 1)
    return pl.pallas_call(
        functools.partial(kernel, 0 if start == 0 else None),
        grid=(count,),
        in_specs=[
            SMEM,
            pl.BlockSpec((1, OWN, SIDE, SIDE), lambda i: (jnp.maximum(i + start - 1, 0), 0, 0, 0)),
            pl.BlockSpec((1, OWN, SIDE, SIDE), lambda i: (0, 0, 0, 0)),
        ],
        out_specs=[pl.BlockSpec((1, c, rows, SIDE), lambda i: (i, 0, 0, 0)) for c in counts],
        out_shape=[jax.ShapeDtypeStruct((count, c, rows, SIDE), F32) for c in counts],
        name="part",
        compiler_params=ROOM,
        cost_estimate=pl.CostEstimate(flops=1 << 20, bytes_accessed=count * 3 << 20, transcendentals=0),
    )(odd, kernels, volume)


def radial_rows(below, own, above, out):
    parts = (below, own, above)

    def tile(i, carry):
        at = pl.ds(pl.multiple_of(i * 8, 8), 8)

        def level(j):
            part, k = (0, j) if j < HALF else (1, j - HALF) if j < HALF + OWN else (2, j - HALF - OWN)
            return parts[part][k, at, :]

        x = [level(j) for j in range(SPAN)]
        for m in range(OWN):
            c = m + HALF
            total = TAPS[0] * x[c]
            for k in range(1, HALF + 1):
                total = total + TAPS[k] * (x[c - k] + x[c + k])
            out[m, at, :] = total
        return carry

    lax.fori_loop(0, out.shape[1] // 8, tile, 0)


def radial_either(odd, near, own, cross, out):
    @pl.when(odd[0] == 0)
    def _():
        radial_rows(cross, own, near, out)

    @pl.when(odd[0] == 1)
    def _():
        radial_rows(near, own, cross, out)


def radial_kernel(odd, *refs):
    radial_either(odd, *[r.at[0] for r in refs])


def radial(odd, near, own, cross):
    count, _, rows, _ = own.shape
    block = rows // 2
    return pl.pallas_call(
        radial_kernel,
        grid=(count, rows // block),
        in_specs=[SMEM]
        + [pl.BlockSpec((1, a.shape[1], block, SIDE), lambda f, i: (f, 0, i, 0)) for a in (near, own, cross)],
        out_specs=pl.BlockSpec((1, OWN, block, SIDE), lambda f, i: (f, 0, i, 0)),
        out_shape=jax.ShapeDtypeStruct(own.shape, F32),
        name="radial",
        compiler_params=ROOM,
        cost_estimate=pl.CostEstimate(
            flops=count * OWN * SPAN * rows * SIDE * 2, bytes_accessed=count * 62 * rows * 512, transcendentals=0
        ),
    )(odd, near, own, cross)


def strips_kernel(glued, odd, pair, picks, near, own, cross, *refs):
    out, rim, edge, rows = refs[-4:]

    def choose(side):
        raw = jnp.where(glued[side] < 2, 1.0, 0.0).astype(F32)
        return picks[side] * raw + picks[side + 2] * (1.0 - raw)

    radial_either(odd, near.at[0], own.at[0], cross.at[0], rim)
    left_high, left_low = split(jnp.concatenate([choose(0), choose(1)], axis=0))
    left = jnp.concatenate([left_high, left_low], axis=0)
    for q in range(OWN):
        base = q * SIDE
        rows[base : base + DEEP, :] = rim[q, :DEEP, :]
        rows[base + SIDE - DEEP : base + SIDE, :] = rim[q, DEEP : 2 * DEEP, :]
        first, second = unpair(rim[q, 2 * DEEP :, :], None)
        rows[base + DEEP : base + UPPER, :] = first
        rows[base + UPPER : base + SIDE - DEEP, :] = second
    for d in range(DEEP):
        edge[pl.ds(d, OWN, stride=DEEP), :] = rows[pl.ds(d, OWN, stride=SIDE), :]
        edge[pl.ds(OWN * DEEP + d, OWN, stride=DEEP), :] = rows[pl.ds(SIDE - 1 - d, OWN, stride=SIDE), :]
    raw = edge[...]
    across = through(raw, pair[...])
    for side in (2, 3):
        at = slice((side - 2) * OWN * DEEP, (side - 1) * OWN * DEEP)
        strip = jnp.where(glued[side] < 2, raw[at], across[at])
        out[:, side, :, :] = strip.reshape(OWN, DEEP, SIDE)
    high, low = split(rows[...])
    both = dot_t(left, high)
    strips = both[: 2 * DEEP] + both[2 * DEEP :] + dot_t(left_high, low)
    for q in range(OWN):
        plane = strips[:, q * SIDE : (q + 1) * SIDE]
        out[q, 0, :, :] = plane[:DEEP]
        out[q, 1, :, :] = plane[DEEP:]


def add_strips(strips, field, halo, place, glued, odd, const):
    arrays = [glued, odd, const["pair"], const["picks"], *halo]
    specs = [SMEM] * 2 + [pl.BlockSpec(a.shape, lambda i, n=a.ndim: (0,) * n) for a in arrays[2:4]]
    specs += [pl.BlockSpec((1,) + a.shape[1:], lambda i: (place, 0, 0, 0)) for a in halo]
    aliases = {}
    if strips is not None:
        aliases = {len(arrays): 0}
        arrays.append(strips)
        specs.append(pl.BlockSpec(memory_space=pl.ANY))
    return pl.pallas_call(
        strips_kernel,
        grid=(1,),
        in_specs=specs,
        out_specs=[
            pl.BlockSpec((OWN, 4, DEEP, SIDE), lambda i: (field, 0, 0, 0)),
            pl.BlockSpec((OWN, RIM, SIDE), lambda i: (0, 0, 0)),
        ],
        out_shape=[
            jax.ShapeDtypeStruct((4 * OWN, 4, DEEP, SIDE), F32),
            jax.ShapeDtypeStruct((OWN, RIM, SIDE), F32),
        ],
        scratch_shapes=[pltpu.VMEM((2 * OWN * DEEP, SIDE), F32), pltpu.VMEM((OWN * SIDE, SIDE), F32)],
        input_output_aliases=aliases,
        name="strips",
        compiler_params=ROOM,
        cost_estimate=pl.CostEstimate(flops=1 << 27, bytes_accessed=3 << 20, transcendentals=0),
    )(*arrays)


def route_kernel(source, fix, ends, corner, flipped, strips, out, patch):
    tiles = out.shape[0]
    group = 4

    def move(i, carry):
        for j in range(8):
            t, s = i * 4 + j // 2, j % 2
            out[t, s, :, :] = strips[source[t * 4 + s], :, :]
        return carry

    lax.fori_loop(0, tiles // 4, move, 0)
    margins = out[:, 0:2, :, :].reshape(tiles * 2 * DEEP, SIDE)
    high, low = split(margins)
    seen = dot_t(ends[...], high) + dot_t(ends[...], low)
    first, last = seen[:DEEP], seen[DEEP:]
    swap = flipped[...] > 0.5
    turned = jnp.concatenate([jnp.where(swap, last, first), jnp.where(swap, first, last)], axis=0)
    groups = tiles // group
    high, low = [
        jnp.concatenate([x[:, g * SIDE : (g + 1) * SIDE] for g in range(groups)], axis=0) for x in split(turned)
    ]
    added = dot(jnp.concatenate([high, low], axis=1), corner[: 2 * SIDE]) + dot(high, corner[2 * SIDE :])
    for g in range(groups):
        for j in range(group):
            block = added[g * 2 * DEEP : (g + 1) * 2 * DEEP, j * SIDE : (j + 1) * SIDE]
            patch[(g * group + j) * 2] = block[:DEEP]
            patch[(g * group + j) * 2 + 1] = block[DEEP:]
    patch[tiles * 2] = jnp.zeros((DEEP, SIDE), F32)

    def mend(i, carry):
        for j in range(8):
            t, s = i * 4 + j // 2, j % 2
            out[t, 2 + s, :, :] = strips[source[t * 4 + 2 + s], :, :] + patch[fix[t * 2 + s], :, :]
        return carry

    lax.fori_loop(0, tiles // 4, mend, 0)


def route(strips, tables, const):
    tiles = strips.shape[0]
    source, fix, flipped = tables
    return pl.pallas_call(
        route_kernel,
        in_specs=[SMEM, SMEM] + [VMEM] * 4,
        out_specs=VMEM,
        out_shape=jax.ShapeDtypeStruct((tiles, 4, DEEP, SIDE), F32),
        scratch_shapes=[pltpu.VMEM((tiles * 2 + 1, DEEP, SIDE), F32)],
        name="route",
        compiler_params=ROOM,
        cost_estimate=pl.CostEstimate(flops=1 << 28, bytes_accessed=4 << 20, transcendentals=0),
    )(source, fix, const["ends"], const["corner"], flipped, strips.reshape(tiles * 4, DEEP, SIDE))


def base_kernel(glued, pair, along, *refs):
    cores, rims = refs[:2], refs[2:6]
    out, rows, across = refs[6:]
    f = pl.program_id(0)
    lane = lanes((SIDE, along.shape[1]))
    south = jnp.where(glued[2] < 2, 1.0, 0.0).astype(F32)
    north = jnp.where(glued[3] < 2, 1.0, 0.0).astype(F32)
    scale = jnp.where(lane < SIDE, 1.0, jnp.where(lane < SIDE + DEEP, south, north))
    left_high, left_low = split(along[...] * scale)
    left = jnp.concatenate([left_high, left_low], axis=0)
    for k in range(4):

        @pl.when(f == k)
        def _():
            for q in range(OWN):
                base = q * SIDE
                rows[base : base + DEEP, :] = rims[k][q, :DEEP, :]
                rows[base + SIDE - DEEP : base + SIDE, :] = rims[k][q, DEEP : 2 * DEEP, :]
                first, second = unpair(rims[k][q, 2 * DEEP :, :], cores[k // 2][0, q])
                rows[base + DEEP : base + UPPER, :] = first
                rows[base + UPPER : base + SIDE - DEEP, :] = second

    across[...] = through(rows[...], pair[...])

    def column(q):
        base = q * SIDE
        own = [rows[base : base + DEEP, :], rows[base + SIDE - DEEP : base + SIDE, :]]
        return jnp.concatenate([across[base : base + SIDE, :]] + own, axis=0)

    for q in range(0, OWN, 2):
        high, low = split(jnp.concatenate([column(q), column(q + 1)], axis=1))
        both = dot(left, high)
        total = both[:SIDE] + both[SIDE:] + dot(left_high, low)
        out[0, q] = total[:, :SIDE]
        out[0, q + 1] = total[:, SIDE:]


def base_lateral(rims, cores, glued, const):
    plane = (1, OWN, SIDE, SIDE)
    return pl.pallas_call(
        base_kernel,
        grid=(4,),
        in_specs=[
            SMEM,
            pl.BlockSpec(const["pair"].shape, lambda i: (0, 0)),
            pl.BlockSpec(const["along"].shape, lambda i: (0, 0)),
            pl.BlockSpec((1, OWN, PAIRS, SIDE), lambda i: (jnp.minimum(i, 1), 0, 0, 0)),
            pl.BlockSpec((1, OWN, PAIRS, SIDE), lambda i: (jnp.maximum(i - 2, 0), 0, 0, 0)),
        ]
        + [pl.BlockSpec((OWN, RIM, SIDE), lambda i: (0, 0, 0))] * 4,
        out_specs=pl.BlockSpec(plane, lambda i: (i, 0, 0, 0)),
        out_shape=jax.ShapeDtypeStruct((4,) + plane[1:], F32),
        scratch_shapes=[pltpu.VMEM((OWN * SIDE, SIDE), F32)] * 2,
        name="base",
        compiler_params=ROOM,
        cost_estimate=pl.CostEstimate(flops=1 << 32, bytes_accessed=9 << 20, transcendentals=0),
    )(glued, const["pair"], const["along"], *cores, *rims)


def turn(code):
    row = lax.broadcasted_iota(jnp.int32, (SIDE, SIDE), 0)
    col = lax.broadcasted_iota(jnp.int32, (SIDE, SIDE), 1)
    return jnp.where(col == jnp.where(code == 1, SIDE - 1 - row, row), 1.0, 0.0).astype(BF16)


def finish_kernel(turned, square, ahead, spread, margins, base, out, below, ways):
    f = pl.program_id(0)
    size = OWN * DEEP

    @pl.when(f == 0)
    def _():
        for side in range(4):
            way = turn(turned[side])
            if side < 2:
                ways[side, 0] = dot(square[0], way).astype(BF16)
                ways[side, 1] = dot(square[1], way).astype(BF16)
            else:
                ways[side, 0] = way

    def margin(side):
        return split(margins[:, side, :, :].reshape(size, SIDE))

    def planes_of(emit):
        sides = []
        for side in (0, 1):
            high, low = margin(side)
            both = dot_t(ways[side].reshape(2 * SIDE, SIDE), high)
            sides.append(both[:SIDE] + both[SIDE:] + dot_t(ways[side, 0], low))
        rows = []
        for side in (2, 3):
            high, low = margin(side)
            way = ways[side, 0]
            rows.append((dot(high, way) + dot(low, way)).reshape(OWN, DEEP, SIDE))
        planes, groups = 4, 4
        parts = []
        for g in range(groups):
            at = slice(g * planes * DEEP, (g + 1) * planes * DEEP)
            parts.append(split(jnp.concatenate([sides[0][:, at], sides[1][:, at]], axis=1)))
        high = jnp.concatenate([x for x, _ in parts], axis=0)
        left = jnp.concatenate([high, jnp.concatenate([x for _, x in parts], axis=0)], axis=1)
        for j in range(0, planes, 2):
            to = slice(j * SIDE, (j + 2) * SIDE)
            added = dot(left, spread[: 2 * SIDE, to])
            for g in range(groups):
                q = g * planes + j
                pairs = [jnp.concatenate([rows[0][k], rows[1][k]], axis=0) for k in (q, q + 1)]
                right, rest = split(jnp.concatenate(pairs, axis=1))
                last = jnp.concatenate([parts[g][0], ahead[...]], axis=1)
                total = added[g * SIDE : (g + 1) * SIDE] + dot(
                    last, jnp.concatenate([spread[2 * SIDE :, to], right, rest, right], axis=0)
                )
                for k in range(2):
                    emit(q + k, total[:, k * SIDE : (k + 1) * SIDE] + base[0, q + k])

    @pl.when(f == 0)
    def _():
        def keep(q, plane):
            below[q] = 1.0 / plane

        planes_of(keep)

    @pl.when(f > 0)
    def _():
        def divide(q, plane):
            out[0, q] = plane * below[q]

        planes_of(divide)


def finish(base, margins, turned, const):
    plane = (1, OWN, SIDE, SIDE)
    return pl.pallas_call(
        finish_kernel,
        grid=(4,),
        in_specs=[
            SMEM,
            pl.BlockSpec(const["square"].shape, lambda i: (0, 0, 0)),
            pl.BlockSpec(const["ahead"].shape, lambda i: (0, 0)),
            pl.BlockSpec(const["spread"].shape, lambda i: (0, 0)),
            pl.BlockSpec((OWN, 4, DEEP, SIDE), lambda i: (i, 0, 0, 0)),
            pl.BlockSpec(plane, lambda i: (i, 0, 0, 0)),
        ],
        out_specs=pl.BlockSpec(plane, lambda i: (jnp.maximum(i - 1, 0), 0, 0, 0)),
        out_shape=jax.ShapeDtypeStruct((3,) + plane[1:], F32),
        scratch_shapes=[pltpu.VMEM(plane[1:], F32), pltpu.VMEM((4, 2, SIDE, SIDE), BF16)],
        name="finish",
        compiler_params=ROOM,
        cost_estimate=pl.CostEstimate(flops=1 << 32, bytes_accessed=9 << 20, transcendentals=0),
    )(turned, const["square"], const["ahead"], const["spread"], margins, base)


NEAR = [(0, 1), (1, 0), (2, 3), (3, 2)]
CROSS = [(1, 2), (2, 1)]


def with_halo(own, near, cross):
    cross = lax.ppermute(cross, "slab", CROSS)
    return lax.ppermute(near, "slab", NEAR), own, cross


def per_device(kernels, volume, neighbours, glued_sides, reversals):
    const = {k: jnp.asarray(v) for k, v in constants().items()}
    tile = lax.axis_index("tile")
    glued = glued_sides[tile]
    turned = reversals[tile]
    odd = (lax.axis_index("slab") % 2)[None]
    tiles = neighbours.shape[0]
    source = (neighbours * 4 + glued_sides).reshape(-1)
    ahead = glued_sides[:, 2:]
    fix = jnp.where(ahead >= 2, neighbours[:, 2:] * 2 + ahead - 2, tiles * 2).reshape(-1)
    flipped = jnp.repeat(reversals[:, :2].astype(F32).reshape(-1), DEEP)[None, :]
    tables = (source, fix, flipped)

    def to_all(x):
        return lax.all_to_all(x, "tile", split_axis=0, concat_axis=0, tiled=True)

    def in_hbm(x):
        return pltpu.with_memory_space_constraint(x, pltpu.HBM)

    source_kernels, source_volume = in_hbm(kernels[0]), in_hbm(volume)
    rims, strips = [], None
    for fields in ((0, 1), (2,), (3,)):
        parts = part_of(rim_kernel, RIM, odd, source_kernels, source_volume, fields)
        halo = with_halo(*parts)
        for place, f in enumerate(fields):
            strips, rim = add_strips(strips, f, halo, place, glued, odd, const)
            rims.append(in_hbm(rim))
    cores = []
    for fields in ((0, 1), (2, 3)):
        parts = part_of(core_kernel, PAIRS, odd, source_kernels, source_volume, fields)
        cores.append(with_halo(*parts))
    routed_in = to_all(strips)
    routed = route(routed_in, tables, const)
    margins = to_all(routed)
    base = in_hbm(base_lateral(rims, [radial(odd, *x) for x in cores], glued, const))
    return finish(base, margins, turned, const)[None]


def solution(mesh):
    placed = (P("tile", None, "slab", None, None), P("tile", "slab", None, None), P(), P(), P())
    return jax.shard_map(
        per_device,
        mesh=mesh,
        in_specs=placed,
        out_specs=P("tile", None, "slab", None, None),
        check_vma=False,
    )
```
